32 devices in a mesh: row: 8 (over z, x), col: 2 (over y), rep: 2 (over core).
Axes of the slice: x: 2, y: 2, z: 4, core: 2. Of those that a mesh axis runs over, the one named last changes fastest.
Arguments:
- rhs_low: float32 [2, 3, 8, 256, 128], P('rep', None, 'row', 'col'), may hold values from -6 to 6
- rhs_top: float32 [8, 256, 128], P('row', 'col'), may hold values from -6 to 6
- inv_low: float32 [2, 3, 8, 256, 256], P('rep', None, 'row', 'col'), as said below
- inv_top: float32 [8, 256, 256], P('row', 'col'), as said below
- blocks: float32 [2, 8, 2, 3, 4, 256, 256], P('rep', 'row', 'col'), may hold values from -0.1875 to 0.1875
- slot_map: int32 [2, 8, 2, 3, 4, 2], P('rep', 'row', 'col'), may hold values from 0 to 3, as said below
Outputs:
- sol_low: float32 [2, 3, 8, 256, 128], P('rep', None, 'row', 'col')
- sol_top: float32 [8, 256, 128], P('row', 'col')
The draws below stay inside these ranges and needn't reach their ends.
Inputs may be any that keep to these rules, and one draw needn't show every extreme that they name: slot_map[s, p, q, l, k] = (t, c): t = 0 marks an empty slot (then c = 0); else 3 >= t > l and c < 4. The live pairs (t, c) of one device and one l are distinct, live slots come before empty ones, every device has at least one live slot for each l, and for each l some device has all 4 slots live. `inv_low`: each block is a dense matrix with a positive diagonal of about one and full off-diagonal entries. `inv_top`: each block is a dense matrix with a positive diagonal of about one and full off-diagonal entries.
All inputs are finite; a program needn't handle non-finite values.
Results may differ from the reference program's by a relative error of at most 0.0003.
Values sent between devices are 32-bit elements; how exact they have to be, the bound alone decides.
A program may use at most 64 MiB of HBM per device.

```python
import math
import jax
import jax.numpy as jnp
from jax import lax

B = 256
R = 128
LOWER = 3
KL = 4
NODES = 8
GRID_COLS = 2
SUBTREES = 2


def inverse_blocks(key, leading):
    key_diag, key_rest = jax.random.split(jax.random.fold_in(key, 11))
    diagonal = jax.random.uniform(key_diag, leading + (B,), jnp.float32, 0.5, 2.0)
    spread = jax.random.normal(key_rest, leading + (B, B), jnp.float32) * (0.6 / math.sqrt(B))
    return spread + diagonal[..., None] * jnp.eye(B, dtype=jnp.float32)


def draw_inv_low(key, part):
    return inverse_blocks(key, (SUBTREES, LOWER, NODES))


def draw_inv_top(key, part):
    return inverse_blocks(key, (NODES,))


def draw_slot_map(key, part):
    col_share = NODES // GRID_COLS
    devices = SUBTREES * NODES * GRID_COLS
    stacks = []
    for height in range(LOWER):
        candidates = (LOWER - height) * col_share
        key_score, key_count, key_full = jax.random.split(jax.random.fold_in(key, 100 + height), 3)
        scores = jax.random.randint(key_score, (devices, candidates), 0, 2 ** 20) * candidates + jnp.arange(candidates, dtype=jnp.int32)
        ranking = jnp.argsort(scores, axis=1)[:, :KL].astype(jnp.int32)
        row_levels = height + 1 + ranking // col_share
        column_ids = ranking % col_share
        counts = jax.random.randint(key_count, (devices,), 1, KL + 1)
        fullest = jax.random.randint(key_full, (), 0, devices)
        counts = jnp.where(jnp.arange(devices) == fullest, KL, counts)
        filled = jnp.arange(KL)[None, :] < counts[:, None]
        stacks.append(jnp.stack([jnp.where(filled, row_levels, 0), jnp.where(filled, column_ids, 0)], axis=-1))
    stacked = jnp.stack(stacks, axis=1)
    return stacked.reshape((SUBTREES, NODES, GRID_COLS, LOWER, KL, 2)).astype(jnp.int32)


def steps_of(rng, shape, cuts, smallest, largest):
    def one(position, blocks):
        draws = jax.random.uniform(jax.random.fold_in(jax.random.fold_in(rng, 6), position), (blocks,), jnp.float32, smallest / len(cuts), largest / len(cuts))
        return jnp.repeat(jnp.exp(draws), shape[position] // blocks).reshape((-1,) + (1,) * (len(shape) - position - 1))

    level = one(*cuts[0])
    for cut in cuts[1:]:
        level = level * one(*cut)
    return level


def noise(key, dims, width, bound, shards=(), kind=jnp.bfloat16):
    factor_of = steps_of(key, dims, shards, -0.22, 0.18) if shards else 1.0
    entries = jax.random.normal(key, dims, jnp.float32) * width * factor_of
    return jnp.minimum(jnp.maximum(entries, -bound), bound).astype(kind)


def setup_inputs(seed: int = 0) -> dict:
    arg_keys = jax.random.split(jax.random.key(seed), 7)
    rhs_low = noise(arg_keys[0], (SUBTREES, LOWER, NODES, B, R), 1.0, 6.0, ((0, 2), (2, 8), (3, 2)), jnp.float32)
    rhs_top = noise(arg_keys[1], (NODES, B, R), 1.0, 6.0, ((0, 8), (1, 2)), jnp.float32)
    inv_low = draw_inv_low(jax.random.fold_in(arg_keys[6], 71), 0)
    inv_top = draw_inv_top(jax.random.fold_in(arg_keys[6], 71), 0)
    blocks = noise(arg_keys[4], (SUBTREES, NODES, GRID_COLS, LOWER, KL, B, B), (B * GRID_COLS * 2) ** -0.5, 0.1875, ((0, 2), (1, 8), (2, 2)), jnp.float32)
    slot_map = draw_slot_map(jax.random.fold_in(arg_keys[6], 71), 0)
    return {"rhs_low": rhs_low, "rhs_top": rhs_top, "inv_low": inv_low, "inv_top": inv_top, "blocks": blocks, "slot_map": slot_map}


def level_terms(block_set, slot_rows, level_sol):
    col_count = block_set.shape[0]
    column_ids = slot_rows[..., 1] * col_count + jnp.arange(col_count, dtype=jnp.int32)[:, None]
    selected = jnp.take(level_sol, column_ids.astype(jnp.int32), axis=0)
    product = jnp.einsum('qkab,qkbr->qkar', block_set, selected, precision=lax.Precision.HIGHEST)
    selector = (slot_rows[..., 0][..., None] == jnp.arange(LOWER + 1, dtype=jnp.int32)).astype(jnp.float32)
    return jnp.einsum('qkt,qkar->tar', selector, product, precision=lax.Precision.HIGHEST)


def reference(rhs_low, rhs_top, inv_low, inv_top, blocks, slot_map):
    highest = lax.Precision.HIGHEST
    rep_count = rhs_low.shape[0]
    node_count = rhs_low.shape[2]
    updates = jnp.zeros((rep_count, LOWER + 1, node_count, B, R), jnp.float32)
    solutions = []
    for height in range(LOWER):
        residue = rhs_low[:, height] - updates[:, height]
        solution = jnp.einsum('spab,spbr->spar', inv_low[:, height], residue, precision=highest)
        solutions.append(solution)
        block_set = blocks[:, :, :, height].reshape((rep_count * node_count,) + blocks.shape[2:3] + blocks.shape[4:])
        slot_rows = slot_map[:, :, :, height].reshape((rep_count * node_count,) + slot_map.shape[2:3] + slot_map.shape[4:])

        def one_row(member):
            return level_terms(block_set[member], slot_rows[member], solution[member // node_count])

        terms = lax.map(one_row, jnp.arange(rep_count * node_count, dtype=jnp.int32))
        terms = terms.reshape((rep_count, node_count, LOWER + 1, B, R))
        updates = updates + jnp.transpose(terms, (0, 2, 1, 3, 4))
    residue = rhs_top - jnp.sum(updates[:, LOWER], axis=0)
    top_rows = jnp.einsum('pab,pbr->par', inv_top, residue, precision=highest)
    return jnp.stack(solutions, axis=1), top_rows
```

```python
import functools
import jax
import jax.numpy as jnp
from jax import lax
from jax.experimental import pallas as pl
from jax.experimental.pallas import tpu as pltpu
from jax.sharding import PartitionSpec as P

MESH = pl.DeviceIdType.MESH


def split(value):
    high = value.astype(jnp.bfloat16)
    low = (value - high.astype(jnp.float32)).astype(jnp.bfloat16)
    return high, low


def dot3(value, right_high, right_low):
    high, low = split(value)
    count = value.shape[0]
    turned = (((1,), (1,)), ((), ()))
    both = jnp.concatenate([high, low], axis=0)
    wide = lax.dot_general(both, right_high, turned, preferred_element_type=jnp.float32)
    rest = lax.dot_general(high, right_low, turned, preferred_element_type=jnp.float32)
    return wide[:count] + (wide[count:] + rest)


def kernel(
    rows, cols, reps, levels, slots, streams,
    rhs_low, rhs_top, inv_low_hbm, inv_top_hbm, blocks_hbm, table_hbm, out_low, out_top,
    table, table_sem, blocks, inverse, right0, rhs, partial, staged, partial_in, top_in, line, inv_high, inv_rest,
    tile_high, tile_rest,
    load_sem, inv_sem, rhs_sem, right_send, right_recv, half_send, half_recv, part_send, part_recv, top_send, top_recv,
    line_send, line_recv, col_send, col_recv, *columns,
):
    row = lax.axis_index("row")
    q = lax.axis_index("col")
    rep = lax.axis_index("rep")
    share = rows // cols
    a = row // cols
    b = row % cols
    part = rhs_top.shape[0]
    depth = partial.shape[2]

    loads = [
        pltpu.make_async_copy(blocks_hbm.at[l], blocks.at[l], load_sem.at[l]) for l in range(levels)
    ]
    inv_loads = [
        pltpu.make_async_copy(inv_low_hbm.at[t] if t < levels else inv_top_hbm, inverse.at[t, q], inv_sem.at[t])
        for t in range(levels + 1)
    ]
    rhs_loads = [pltpu.make_async_copy(rhs_low.at[0], right0.at[q], rhs_sem.at[0])]
    for t in range(1, levels + 1):
        rhs_loads.append(
            pltpu.make_async_copy(rhs_low.at[t] if t < levels else rhs_top, rhs.at[t], rhs_sem.at[t])
        )
    for load in [rhs_loads[0], inv_loads[0], loads[0]] + rhs_loads[1:] + inv_loads[1:] + loads[1:]:
        load.start()

    table_load = pltpu.make_async_copy(table_hbm, table, table_sem)
    table_load.start()
    col_peers = [lax.rem(q + d, cols) for d in range(1, cols)]
    rep_peers = [lax.rem(rep + d, reps) for d in range(1, reps)]

    barrier = pltpu.get_barrier_semaphore()
    count = 0
    for dr in range(cols):
        for dc in range(cols):
            if dr or dc:
                pl.semaphore_signal(
                    barrier, inc=1, device_id_type=MESH,
                    device_id={"row": a * cols + lax.rem(b + dr, cols), "col": lax.rem(q + dc, cols)},
                )
                count += 1
    for d in range(1, share):
        pl.semaphore_signal(
            barrier, inc=1, device_id_type=MESH,
            device_id={"row": lax.rem(a + d, share) * cols + b},
        )
        count += 1
    for peer in rep_peers:
        pl.semaphore_signal(barrier, inc=1, device_id_type=MESH, device_id={"rep": peer})
        count += 1
    pl.semaphore_wait(barrier, count)

    started = []
    conditional = []

    def send(src, dst, send_sem, recv_sem, device):
        return pltpu.make_async_remote_copy(
            src_ref=src, dst_ref=dst, send_sem=send_sem, recv_sem=recv_sem,
            device_id=device, device_id_type=MESH,
        )

    def settle():
        for copy in started:
            copy.wait_send()
        started.clear()

        @pl.when(q != b)
        def _():
            for copy in conditional:
                copy.wait_send()

        conditional.clear()

    def go(copy):
        copy.start()
        started.append(copy)

    def begin(d, source, peer):
        return send(rhs_low.at[0], right0.at[source], right_send.at[d], right_recv.at[source], {"col": peer})

    def share_half(t, d, source, peer):
        return send(
            inv_low_hbm.at[t] if t < levels else inv_top_hbm, inverse.at[t, source], half_send.at[t, d],
            half_recv.at[t, source], {"col": peer},
        )

    def share_inverse(t):
        for d, peer in enumerate(col_peers):
            go(share_half(t, d, q, peer))

    for d, peer in enumerate(col_peers):
        go(begin(d, q, peer))
    for t in range(1, levels):
        share_inverse(t)

    def take_inverse(t):
        inv_loads[t].wait()
        if t == 0:
            high, low = split(inverse[t, q])
            inv_high[t, q] = high
            inv_rest[t, q] = low
        else:
            for d, peer in enumerate(col_peers):
                share_half(t, d, peer, peer).wait_recv()
            high, low = split(inverse[t])
            inv_high[t] = high
            inv_rest[t] = low

    def apply_inverse(t, s, total):
        size = cols * part
        solved = dot3(total, inv_high[t].reshape(size, size), inv_rest[t].reshape(size, size))
        for j in range(cols):
            staged[t, s, j] = solved[:, j * part:(j + 1) * part]

    def take_rhs(t):
        rhs_loads[t].wait()
        turned = rhs[t].T
        if t == levels:
            turned = jnp.where(rep == 0, turned, 0.0)
        spaced = jnp.concatenate([jnp.where(q == j, turned, 0.0) for j in range(cols)], axis=1)
        for s in range(streams):
            partial[t, s] = spaced[s * depth:(s + 1) * depth]

    take_inverse(0)
    table_load.wait()

    def order(i, here):
        low_side = jnp.where(i >= here, i + 1, i)
        mirror = share - 1 - here
        high_side = share - 1 - jnp.where(i >= mirror, i + 1, i)
        return jnp.where(2 * here < share, low_side, high_side)

    def hop(t, s, source, d, target, peer):
        return send(
            staged.at[t, s, target], partial_in.at[t, source, s], part_send.at[t, d, s], part_recv.at[t, source, s],
            {"col": peer},
        )

    def exchange(t, s):
        for d, peer in enumerate(col_peers):
            go(hop(t, s, q, d, peer, peer))

    def collect(t, s):
        total = staged[t, s, q]
        for d, peer in enumerate(col_peers):
            hop(t, s, peer, d, peer, peer).wait_recv()
            total = total + partial_in[t, peer, s]
        return total

    def lift(s, d, peer):
        return send(partial.at[levels, s], top_in.at[d, s], top_send.at[d, s], top_recv.at[d, s], {"rep": peer})

    def along(l, s, i, source, target):
        return send(
            line.at[l, s, source], line.at[l, s, source], line_send.at[l, s, i], line_recv.at[l, s, source],
            {"row": target * cols + b},
        )

    def spread(l, s, c, index):
        for d in range(cols):
            copy = send(
                line.at[l, s, c], columns[l * streams + s].at[c, q], col_send.at[l, s, index, d],
                col_recv.at[l, s, c, q],
                {"row": a * cols + lax.rem(b + d, cols), "col": b},
            )
            if d == 0:
                pl.when(q != b)(copy.start)
                conditional.append(copy)
            else:
                go(copy)

        @pl.when(q == b)
        def _():
            columns[l * streams + s][c, q] = line[l, s, c]

    residue0 = None
    for l in range(levels):
        pieces = []
        mark, mark2 = len(started), len(conditional)
        for s in range(streams):
            if l == 0:
                if s == 0:
                    for d, peer in enumerate(col_peers):
                        begin(d, peer, peer).wait_recv()
                    rhs_loads[0].wait()
                    residue0 = right0[...].reshape(part * cols, right0.shape[2]).T
                residue = residue0[s * depth:(s + 1) * depth]
                solved = dot3(residue, inv_high[0, q], inv_rest[0, q])
            else:
                solved = collect(l, s)
            line[l, s, a] = solved
            for i in reversed(range(share - 1)):
                go(along(l, s, i, a, order(i, a)))
            spread(l, s, a, share - 1)
            pieces.append(solved)
        if l == min(1, levels - 1):
            share_inverse(levels)
        loads[l].wait()
        for k in range(slots):
            high, low = split(blocks[l, k])
            tile_high[k] = high
            tile_rest[k] = low
        for s in range(streams):
            for i in range(share - 1):
                c = order(i, a)
                along(l, s, i, c, c).wait_recv()
                spread(l, s, c, i)
        current, waiting = started[mark:], conditional[mark2:]
        del started[mark:], conditional[mark2:]
        settle()
        started.extend(current)
        conditional.extend(waiting)
        out_low[l] = jnp.concatenate(pieces, axis=0).T
        take_inverse(l + 1)
        if l == 0:
            for t in range(1, levels + 1):
                take_rhs(t)
        later = []

        def add(t, s, products):
            total = partial[t, s]
            for k in range(slots):
                total = total - jnp.where(table[l, 0, k] == t, products[k], 0.0)
            partial[t, s] = total

        for s in range(streams):
            for c in range(share):
                for source in range(cols):
                    copy = send(
                        line.at[l, s, c], columns[l * streams + s].at[c, source], col_send.at[l, s, c, 0],
                        col_recv.at[l, s, c, source],
                        {"row": a * cols + q, "col": lax.rem(q + 1, cols)},
                    )
                    pl.when(jnp.logical_or(b != q, source != q))(copy.wait_recv)
            products = []
            for k in range(slots):
                found = columns[l * streams + s][table[l, 1, k]]
                picked = jnp.concatenate([found[j] for j in range(cols)], axis=1)
                products.append(dot3(picked, tile_high[k], tile_rest[k]))
            later.append((s, products))
            add(l + 1, s, products)
            if l + 1 < levels:
                apply_inverse(l + 1, s, partial[l + 1, s])
                exchange(l + 1, s)
            if l + 1 == levels:
                for d, peer in enumerate(rep_peers):
                    go(lift(s, d, peer))
        for s, products in later:
            for t in range(l + 2, levels + 1):
                add(t, s, products)

    mark = len(started)
    for s in range(streams):
        total = partial[levels, s]
        for d, peer in enumerate(rep_peers):
            lift(s, d, peer).wait_recv()
            total = total + top_in[d, s]
        apply_inverse(levels, s, total)
        exchange(levels, s)
    current = started[mark:]
    del started[mark:]
    settle()
    started.extend(current)
    pieces = []
    for s in range(streams):
        pieces.append(collect(levels, s))
    out_top[...] = jnp.concatenate(pieces, axis=0).T

    settle()


def per_device(rows, cols, reps, rhs_low, rhs_top, inv_low, inv_top, blocks, slot_map):
    rhs_low, rhs_top = rhs_low[0, :, 0], rhs_top[0]
    inv_low, inv_top = inv_low[0, :, 0], inv_top[0]
    blocks, table = blocks[0, 0, 0], jnp.swapaxes(slot_map[0, 0, 0], 1, 2)
    levels, slots, size = blocks.shape[:3]
    rhs_low, rhs_top, inv_low, inv_top, blocks, table = [
        pltpu.with_memory_space_constraint(x, pltpu.HBM) for x in (rhs_low, rhs_top, inv_low, inv_top, blocks, table)
    ]
    part, width = rhs_top.shape
    share = rows // cols
    vmem = pl.BlockSpec(memory_space=pltpu.VMEM)
    hbm = pl.BlockSpec(memory_space=pltpu.HBM)
    streams = 2
    depth = width // streams
    dma = pltpu.SemaphoreType.DMA
    f32, bf16 = jnp.float32, jnp.bfloat16
    sol_low, sol_top = pl.pallas_call(
        functools.partial(kernel, rows, cols, reps, levels, slots, streams),
        out_shape=(
            jax.ShapeDtypeStruct((levels, part, width), f32),
            jax.ShapeDtypeStruct((part, width), f32),
        ),
        in_specs=[hbm, hbm, hbm, hbm, hbm, hbm],
        out_specs=(vmem, vmem),
        scratch_shapes=[
            pltpu.SMEM(table.shape, jnp.int32),
            dma(()),
            pltpu.VMEM((levels, slots, size, size), f32),
            pltpu.VMEM((levels + 1, cols, part, size), f32),
            pltpu.VMEM((cols, part, width), f32),
            pltpu.VMEM((levels + 1, part, width), f32),
            pltpu.VMEM((levels + 1, streams, depth, size), f32),
            pltpu.VMEM((levels + 1, streams, cols, depth, part), f32),
            pltpu.VMEM((levels + 1, cols, streams, depth, part), f32),
            pltpu.VMEM((reps - 1, streams, depth, size), f32),
            pltpu.VMEM((levels, streams, share, depth, part), f32),
            pltpu.VMEM((levels + 1, cols, part, size), bf16),
            pltpu.VMEM((levels + 1, cols, part, size), bf16),
            pltpu.VMEM((slots, size, size), bf16),
            pltpu.VMEM((slots, size, size), bf16),
            dma((levels,)),
            dma((levels + 1,)),
            dma((levels + 1,)),
            dma((cols - 1,)),
            dma((cols,)),
            dma((levels + 1, cols - 1)),
            dma((levels + 1, cols)),
            dma((levels + 1, cols - 1, streams)),
            dma((levels + 1, cols, streams)),
            dma((reps - 1, streams)),
            dma((reps - 1, streams)),
            dma((levels, streams, share - 1)),
            dma((levels, streams, share)),
            dma((levels, streams, share, cols)),
            dma((levels, streams, share, cols)),
        ]
        + [pltpu.VMEM((share, cols, depth, part), f32)] * (levels * streams),
        compiler_params=pltpu.CompilerParams(
            collective_id=0, has_side_effects=True, vmem_limit_bytes=48 * 1024 * 1024
        ),
    )(rhs_low, rhs_top, inv_low, inv_top, blocks, table)
    return (sol_low[None, :, None], sol_top[None])


def solution(mesh):
    in_specs = (
        P("rep", None, "row", "col", None),
        P("row", "col", None),
        P("rep", None, "row", "col", None),
        P("row", "col", None),
        P("rep", "row", "col", None, None, None, None),
        P("rep", "row", "col", None, None, None),
    )
    out_specs = (P("rep", None, "row", "col", None), P("row", "col", None))
    body = functools.partial(per_device, mesh.shape["row"], mesh.shape["col"], mesh.shape["rep"])
    return jax.shard_map(body, mesh=mesh, in_specs=in_specs, out_specs=out_specs, check_vma=False)
```
